32 devices in a mesh: subj: 8 (over z, y), space: 4 (over x, core).
Axes of the slice: x: 2, y: 2, z: 4, core: 2. Of those that a mesh axis runs over, the one named last changes fastest.
Arguments:
- template: float32 [4, 32, 4096], P(None, 'space', 'subj'), may hold values from -6 to 6
- images: bfloat16 [8, 32, 4096], P('subj', 'space'), may hold values from -6 to 6
- speeds: float32 [8, 3, 32, 4096], P('subj', None, 'space'), may hold values from 0.02 to 0.3
- direction: int32 [8, 3, 32, 4096], P('subj', None, 'space'), may hold values from 0 to 1
- membership: int32 [8, 1], P('subj'), may hold values from 0 to 3
Outputs:
- new_velocity: float32 [8, 3, 32, 4096], P('subj', None, 'space')
- new_template: float32 [4, 32, 4096], P(None, 'space', 'subj')
The draws below stay inside these ranges and needn't reach their ends.
Inputs may be any that keep to these rules, and one draw needn't show every extreme that they name: `membership`: every one of the 4 groups has at least one subject, and group sizes differ.
All inputs are finite; a program needn't handle non-finite values.
Results may differ from the reference program's by a relative error of at most 0.00035.
Values sent between devices are 32-bit elements; how exact they have to be, the bound alone decides.
A program may use at most 64 MiB of HBM per device.

```python
import math
import jax
import jax.numpy as jnp
from jax import lax

GROUPS = 4
NZ = 16
NY = 256
STEPS = 4
PASSES = 4
PLANE = 4096
SUBJECTS = 8
NX = 32


def touch_ends(array, stream_key, smallest, top_value):
    spot = [jax.random.randint(jax.random.fold_in(stream_key, axis), (), 0, length) for axis, length in enumerate(array.shape)]
    longest = array.shape.index(max(array.shape))
    next_to = spot[:longest] + [(spot[longest] + 1) % array.shape[longest]] + spot[longest + 1:]
    return array.at[tuple(spot)].set(smallest).at[tuple(next_to)].set(top_value)


def strengthened(array, stream_key, source, target, shards_of, factor):
    def block_of(dim):
        return (jnp.arange(array.shape[dim]) // (array.shape[dim] // shards_of)).reshape((-1,) + (1,) * (array.ndim - 1 - dim))

    first = jax.random.permutation(stream_key, shards_of)[block_of(target)]
    other_side = (block_of(target) + shards_of // 2) % shards_of
    return jnp.where((block_of(source) == first) | (block_of(source) == other_side), factor * array, array)


def shard_levels(own_key, dims, split, smallest, high):
    def one(position, parts):
        heights = jax.random.uniform(jax.random.fold_in(jax.random.fold_in(own_key, 6), position), (parts,), jnp.float32, smallest / len(split), high / len(split))
        return jnp.repeat(jnp.exp(heights), dims[position] // parts).reshape((-1,) + (1,) * (len(dims) - position - 1))

    level = one(*split[0])
    for cut in split[1:]:
        level = level * one(*cut)
    return level


def picks_of(own_key, rows, amount, top, lift):
    sequence = jax.random.permutation(jax.random.fold_in(own_key, 1), amount)
    favour = sequence
    for power in range(3):
        favour = favour * favour // amount
    favour = favour * lift // amount
    chance = jax.random.randint(jax.random.fold_in(own_key, 2), (rows, amount), 0, 4096) + favour
    holders = jax.random.permutation(jax.random.fold_in(own_key, 3), rows)[jnp.arange(amount) % rows]
    chance = jnp.where(jnp.arange(rows)[:, None] == holders[None, :], 1 << 14, chance)
    merit = chance * amount + jnp.arange(amount)
    return lax.top_k(merit.astype(jnp.int32), top)[1].astype(jnp.int32)


def bell_draw(key, shape, scale, reach, pieces=(), held_as=jnp.bfloat16):
    level = shard_levels(key, shape, pieces, -0.22, 0.18) if pieces else 1.0
    values = jax.random.normal(key, shape, jnp.float32) * scale * level
    return jnp.minimum(jnp.maximum(values, -reach), reach).astype(held_as)


def bell_draw_with(key, dims, width, limit, shards, heavy, kind=jnp.bfloat16):
    result = width * jax.random.normal(key, dims, jnp.float32)
    if shards:
        result = result * shard_levels(key, dims, shards, -0.22, 0.18)
    return jnp.clip(strengthened(result, jax.random.fold_in(key, 3), *heavy), -limit, limit).astype(kind)


def setup_inputs(seed: int = 0) -> dict:
    arg_keys = jax.random.split(jax.random.key(seed), 6)
    template = bell_draw(arg_keys[0], (GROUPS, NX, PLANE), 1.0, 6.0, ((1, 4), (2, 8)), jnp.float32)
    images = bell_draw_with(arg_keys[1], (SUBJECTS, NX, PLANE), 1.0, 6.0, ((0, 8), (1, 4)), (0, 2, 8, 2.0))
    speeds = jnp.clip(jnp.exp(math.log(0.3) - 2.7080503 * jax.random.uniform(arg_keys[2], (SUBJECTS, 3, NX, PLANE), jnp.float32) ** shard_levels(arg_keys[2], (SUBJECTS, 3, NX, PLANE), ((0, 8), (2, 4)), -0.2, 0.2)), 0.02, 0.3)
    direction = touch_ends(jax.random.randint(arg_keys[3], (SUBJECTS, 3, NX, PLANE), 0, 2), jax.random.fold_in(arg_keys[3], 1), 0, 1).astype(jnp.int32)
    membership = picks_of(arg_keys[4], SUBJECTS, GROUPS, 1, 4096)
    return {"template": template, "images": images, "speeds": speeds, "direction": direction, "membership": membership}


update_rate = 0.5


def neighbour(values, dimension, stride):
    length = values.shape[dimension]
    margins = [(0, 0)] * values.ndim
    margins[dimension] = (1, 1)
    padded = jnp.pad(values, margins)
    return lax.slice_in_dim(padded, 1 + stride, 1 + stride + length, axis=dimension)


def pad_edge(values, dimension):
    margins = [(0, 0)] * values.ndim
    margins[dimension] = (1, 1)
    return jnp.pad(values, margins)


def advect(extended, velocity, forward):
    center = extended[:, 1:-1]
    across = jnp.where(forward[:, 0], center - extended[:, :-2], extended[:, 2:] - center)
    depth_diff = jnp.where(forward[:, 1], center - neighbour(center, 2, -1), neighbour(center, 2, 1) - center)
    row_diff = jnp.where(forward[:, 2], center - neighbour(center, 3, -1), neighbour(center, 3, 1) - center)
    return center - (velocity[:, 0] * across + velocity[:, 1] * depth_diff + velocity[:, 2] * row_diff)


def slopes(extended):
    center = extended[:, 1:-1]
    gradients = jnp.stack([
        0.5 * (extended[:, 2:] - extended[:, :-2]),
        0.5 * (neighbour(center, 2, 1) - neighbour(center, 2, -1)),
        0.5 * (neighbour(center, 3, 1) - neighbour(center, 3, -1))], axis=1)
    return center, gradients


def relax(extended):
    center = extended[:, :, 1:-1]
    beside_all = extended[:, :, 2:] + extended[:, :, :-2]
    beside_all = beside_all + neighbour(center, 3, 1) + neighbour(center, 3, -1)
    beside_all = beside_all + neighbour(center, 4, 1) + neighbour(center, 4, -1)
    return center + 0.125 * (beside_all - 6.0 * center)


def reference(template, images, speeds, direction, membership):
    onehot = (membership == jnp.arange(GROUPS, dtype=jnp.int32)[None, :]).astype(jnp.float32)
    counts = jnp.sum(onehot, axis=0)
    templates_flat = template.reshape(GROUPS, NX * PLANE)

    def one_subject(bundle):
        subject_image, subject_speed, subject_dirs, member = bundle
        intensity = subject_image.astype(jnp.float32).reshape(1, NX, NZ, NY)
        forward = subject_dirs.reshape(1, 3, NX, NZ, NY) == 1
        velocity = ((2 * subject_dirs - 1).astype(jnp.float32) * subject_speed).reshape(1, 3, NX, NZ, NY)
        for repeat in range(STEPS):
            intensity = advect(pad_edge(intensity, 1), velocity, forward)
        center, gradients = slopes(pad_edge(intensity, 1))
        chosen = jnp.einsum('g,gp->p', member, templates_flat, precision=lax.Precision.HIGHEST).reshape(1, NX, NZ, NY)
        forcing = (center - chosen)[:, None] * gradients
        for repeat in range(PASSES):
            forcing = relax(pad_edge(forcing, 2))
        updated = velocity - update_rate * forcing
        return center.reshape(NX, PLANE), updated.reshape(3, NX, PLANE)

    warped, velocities = lax.map(one_subject, (images, speeds, direction, onehot))
    group_sums = jnp.einsum('sg,sxp->gxp', onehot, warped, precision=lax.Precision.HIGHEST)
    return velocities, group_sums / counts[:, None, None]
```

```python
import functools

import jax
import jax.numpy as jnp
from jax import lax
from jax.experimental import pallas as pl
from jax.experimental.pallas import tpu as pltpu
from jax.sharding import PartitionSpec as P

NY = 256
STEPS = 4
PASSES = 4
LANES = 128
SLAB = 8
NH = NY // LANES
ROWS = 3 * SLAB
TOP = SLAB
END = 2 * SLAB
MESH = pl.DeviceIdType.MESH

update_rate = 0.5


def to(axis, index):
    return {"device_id": {axis: index}, "device_id_type": MESH}


def partner(s, k):
    t = s
    bit = 1
    while bit <= k:
        if k & bit:
            t = t + bit - 2 * bit * lax.rem(s // bit, 2)
        bit *= 2
    return t


def beside_in_row(x, depth):
    count, rows, _ = x.shape
    grid = x.reshape(depth, NH, rows, LANES)
    lane = lax.broadcasted_iota(jnp.int32, (depth, rows, LANES), 2)
    up = pltpu.roll(grid, 1, 3)
    down = pltpu.roll(grid, LANES - 1, 3)
    zero = jnp.zeros((depth, rows, LANES), jnp.float32)
    before, after = [], []
    for h in range(NH):
        before.append(jnp.where(lane == 0, up[:, h - 1] if h else zero, up[:, h]))
        after.append(
            jnp.where(lane == LANES - 1, down[:, h + 1] if h + 1 < NH else zero, down[:, h])
        )
    return (
        jnp.stack(before, axis=1).reshape(count, rows, LANES),
        jnp.stack(after, axis=1).reshape(count, rows, LANES),
    )


def kernel(
    groups, slabs, people, chunks, piece, depth,
    template_any, images_any, speeds_any, direction_any, membership_any,
    out_velocity, out_template,
    template, images, speeds, direction, membership, load,
    field_a, field_b, warped, velocity, force_a, force_b, chosen, chosen_out, gathered, members,
    halo_send, halo_recv, member_send, member_recv, mate_send, pick_send, pick_recv, warp_send, warp_recv,
):
    p = lax.axis_index("space")
    s = lax.axis_index("subj")
    has_left = p > 0
    has_right = p < slabs - 1
    is_odd = lax.rem(p, 2) == 1
    is_even = jnp.logical_not(is_odd)
    far_left = has_left & is_even
    far_right = has_right & is_odd
    barrier = pltpu.get_barrier_semaphore()

    @pl.when(has_left)
    def _():
        pl.semaphore_signal(barrier, 1, **to("space", p - 1))

    @pl.when(has_right)
    def _():
        pl.semaphore_signal(barrier, 1, **to("space", p + 1))

    for k in range(1, people):
        pl.semaphore_signal(barrier, 1, **to("subj", partner(s, k)))

    loads = [
        pltpu.make_async_copy(source, target, load.at[i])
        for i, (source, target) in enumerate(
            ((membership_any, membership), (images_any, images), (speeds_any, speeds), (direction_any, direction))
        )
    ] + [
        pltpu.make_async_copy(
            template_any.at[:, :, pl.ds(j * LANES, LANES)],
            template.at[:, j, pl.ds(TOP, SLAB)],
            load.at[4 + j],
        )
        for j in range(piece)
    ]
    for copy in loads:
        copy.start()
    inner = slice(NH, NH + chunks)
    wide = depth * NH
    blocks = chunks // wide

    edge = jnp.zeros((NH, ROWS, LANES), jnp.float32)
    for field in (field_a, field_b, warped):
        field[0:NH] = edge
        field[NH + chunks :] = edge
    for field in (force_a, force_b):
        for c in range(3):
            field[c, 0:NH] = edge
            field[c, NH + chunks :] = edge
    outside = jnp.zeros((chunks, SLAB, LANES), jnp.float32)

    def blank(rows):
        field_a[inner, rows] = outside
        warped[inner, rows] = outside
        template[:, :, rows] = jnp.zeros((groups, piece, SLAB, LANES), jnp.float32)
        for c in range(3):
            velocity[c, :, rows] = outside

    @pl.when(jnp.logical_not(has_left))
    def _():
        blank(slice(0, TOP))
        chosen[:, 0:PASSES] = outside[:, 0:PASSES]

    @pl.when(jnp.logical_not(has_right))
    def _():
        blank(slice(END, ROWS))
        chosen[:, PASSES + SLAB :] = outside[:, 0:PASSES]

    @pl.when(has_left & is_odd)
    def _():
        template[:, :, 0:TOP] = jnp.zeros((groups, piece, SLAB, LANES), jnp.float32)

    @pl.when(has_right & is_even)
    def _():
        template[:, :, END:ROWS] = jnp.zeros((groups, piece, SLAB, LANES), jnp.float32)

    for copy in loads:
        copy.wait()
    def unpack(i, _):
        start = pl.multiple_of(i * wide * LANES, LANES)
        block = images[0, :, pl.ds(start, wide * LANES)].astype(jnp.float32)
        for j in range(wide):
            field_a[NH + i * wide + j, TOP:END] = block[:, j * LANES : (j + 1) * LANES]
        for c in range(3):
            sign = (2 * direction[0, c, :, pl.ds(start, wide * LANES)] - 1).astype(jnp.float32)
            signed = sign * speeds[0, c, :, pl.ds(start, wide * LANES)]
            for j in range(wide):
                velocity[c, i * wide + j, TOP:END] = signed[:, j * LANES : (j + 1) * LANES]
        return 0

    lax.fori_loop(0, blocks, unpack, 0)
    members[s] = jnp.broadcast_to(membership[...], (1, LANES))
    near = jnp.where(has_left, 1, 0) + jnp.where(has_right, 1, 0)
    pl.semaphore_wait(barrier, near + people - 1)

    def halo(number, cut, width, with_left=has_left, with_right=has_right):
        def copy(side, source, target, index):
            return pltpu.make_async_remote_copy(
                src_ref=cut(source), dst_ref=cut(target),
                send_sem=halo_send.at[2 * number + side], recv_sem=halo_recv.at[2 * number + side],
                **to("space", index),
            )

        left = copy(0, TOP, END, p - 1)
        right = copy(1, END - width, TOP - width, p + 1)

        def both(to_left, to_right):
            @pl.when(with_left)
            def _():
                to_left()

            @pl.when(with_right)
            def _():
                to_right()

        start = lambda: both(left.start, right.start)
        sent = lambda: both(left.wait_send, right.wait_send)
        landed = lambda: both(right.wait_recv, left.wait_recv)
        return start, sent, landed

    def member_copy(k):
        return pltpu.make_async_remote_copy(
            src_ref=members.at[s], dst_ref=members.at[s],
            send_sem=member_send.at[k], recv_sem=member_recv.at[k],
            **to("subj", partner(s, k)),
        )

    def mate_copy(k):
        t = partner(s, k)
        return pltpu.make_async_remote_copy(
            src_ref=members.at[t], dst_ref=members.at[t],
            send_sem=mate_send.at[k], recv_sem=member_recv.at[k],
            **to("space", p + 1 - 2 * lax.rem(p, 2)),
        )

    def pick_copies(k):
        t = partner(s, k)

        def over(first, rows):
            return pltpu.make_async_remote_copy(
                src_ref=chosen_out.at[t, :, pl.ds(first, rows)],
                dst_ref=chosen.at[pl.ds(s * piece, piece), pl.ds(first, rows)],
                send_sem=pick_send.at[k], recv_sem=pick_recv.at[k],
                **to("subj", t),
            )

        return (
            (far_left, over(0, PASSES + SLAB)),
            (far_right, over(PASSES, PASSES + SLAB)),
            (jnp.logical_not(far_left | far_right), over(PASSES, SLAB)),
        )

    def pick_all(k, act):
        for condition, copy in pick_copies(k):
            pl.when(condition)(functools.partial(act, copy))

    def pick(t):
        mine = jnp.broadcast_to(members[t], (2 * SLAB, LANES))
        for j in range(piece):
            total = jnp.zeros((2 * SLAB, LANES), jnp.float32)
            for g in range(groups):
                total = jnp.where(mine == g, template[g, j, TOP - PASSES : END + PASSES], total)
            chosen_out[t, j] = total

    def warp_copy(k):
        t = partner(s, k)
        return pltpu.make_async_remote_copy(
            src_ref=warped.at[pl.ds(NH + t * piece, piece), pl.ds(TOP, SLAB)],
            dst_ref=gathered.at[s],
            send_sem=warp_send.at[k], recv_sem=warp_recv.at[k],
            **to("subj", t),
        )

    image_halo = halo(0, lambda r: field_a.at[pl.ds(NH, chunks), pl.ds(r, STEPS)], STEPS)
    speed_halo = halo(1, lambda r: velocity.at[:, :, pl.ds(r, STEPS - 1)], STEPS - 1)
    warp_halo = halo(2, lambda r: warped.at[pl.ds(NH, chunks), pl.ds(r, PASSES + 1)], PASSES + 1)
    piece_halo = halo(
        3, lambda r: template.at[:, :, pl.ds(r, PASSES)], PASSES, far_left, far_right
    )
    pick_halo = halo(
        4, lambda r: chosen.at[:, pl.ds(r - PASSES, PASSES)], PASSES,
        has_left & is_odd, has_right & is_even,
    )

    order = range(1, people)

    @pl.when(is_odd)
    def _():
        for k in order:
            member_copy(k).start()

    piece_halo[0]()
    image_halo[0]()
    speed_halo[0]()
    piece_halo[2]()
    for k in order:
        member_copy(k).wait_recv()

        @pl.when(is_odd)
        def _():
            mate_copy(k).start()

        pick(partner(s, k))
        pick_all(k, lambda copy: copy.start())
    pick(s)
    own = pl.ds(PASSES, SLAB)
    chosen[pl.ds(s * piece, piece), own] = chosen_out[s, :, own]

    @pl.when(far_left)
    def _():
        chosen[pl.ds(s * piece, piece), 0:PASSES] = chosen_out[s, :, 0:PASSES]

    @pl.when(far_right)
    def _():
        chosen[pl.ds(s * piece, piece), PASSES + SLAB :] = chosen_out[s, :, PASSES + SLAB :]

    image_halo[2]()
    speed_halo[2]()

    def advect(source, target, first, rows):
        def block(i, _):
            at = i * wide
            center = source[pl.ds(NH + at, wide), first : first + rows]

            def x(shift):
                return source[pl.ds(NH + at, wide), first + shift : first + shift + rows]

            def z(shift):
                return source[pl.ds(NH + at + shift * NH, wide), first : first + rows]

            def v(c):
                return velocity[c, pl.ds(at, wide), first : first + rows]

            before, after = beside_in_row(center, depth)
            moved = jnp.zeros_like(center)
            for c, (low, high) in enumerate(((x(-1), x(1)), (z(-1), z(1)), (before, after))):
                speed = v(c)
                moved = moved + speed * jnp.where(speed > 0.0, center - low, high - center)
            target[pl.ds(NH + at, wide), first : first + rows] = center - moved
            return 0

        lax.fori_loop(0, blocks, block, 0)

    reach = SLAB // 2
    fields = (field_a, field_b)
    for step in range(STEPS):
        if step == 1:
            image_halo[1]()
        if step < STEPS - 1:
            advect(fields[step % 2], fields[(step + 1) % 2], TOP - reach, 2 * SLAB)
        else:
            advect(fields[step % 2], warped, TOP, SLAB)

    warp_halo[0]()
    for k in reversed(order):
        warp_copy(k).start()
    gathered[s] = warped[pl.ds(NH + s * piece, piece), TOP:END]

    for k in order:
        pick_all(k, lambda copy: copy.wait_recv())
    pick_halo[0]()
    warp_halo[2]()
    pick_halo[2]()

    first, rows = TOP - reach, 2 * SLAB

    def push(i, _):
        at = i * wide
        center = warped[pl.ds(NH + at, wide), first : first + rows]
        before, after = beside_in_row(center, depth)
        half = 0.5 * (center - chosen[pl.ds(at, wide)])
        up = warped[pl.ds(NH + at, wide), first - 1 : first - 1 + rows]
        down = warped[pl.ds(NH + at, wide), first + 1 : first + 1 + rows]
        low = warped[pl.ds(at, wide), first : first + rows]
        high = warped[pl.ds(2 * NH + at, wide), first : first + rows]
        here = pl.ds(NH + at, wide)
        force_a[0, here, first : first + rows] = half * (down - up)
        force_a[1, here, first : first + rows] = half * (high - low)
        force_a[2, here, first : first + rows] = half * (after - before)
        return 0

    lax.fori_loop(0, blocks, push, 0)

    row = lax.broadcasted_iota(jnp.int32, (1, rows, LANES), 1) + first
    lowest = jnp.where(has_left, 0, TOP)
    highest = jnp.where(has_right, ROWS, END)
    kept = (row >= lowest) & (row < highest)

    def relaxed(source, c, at, first, rows):
        center = source[c, pl.ds(NH + at, wide), first : first + rows]
        before, after = beside_in_row(center, depth)
        total = before + after
        total = total + source[c, pl.ds(NH + at, wide), first - 1 : first - 1 + rows]
        total = total + source[c, pl.ds(NH + at, wide), first + 1 : first + 1 + rows]
        total = total + source[c, pl.ds(at, wide), first : first + rows]
        total = total + source[c, pl.ds(2 * NH + at, wide), first : first + rows]
        return 0.25 * center + 0.125 * total

    forces = (force_a, force_b)
    for number in range(PASSES - 1):
        source, target = forces[number % 2], forces[(number + 1) % 2]

        def smooth(i, _, source=source, target=target):
            at = i * wide
            for c in range(3):
                value = relaxed(source, c, at, first, rows)
                target[c, pl.ds(NH + at, wide), first : first + rows] = jnp.where(
                    jnp.broadcast_to(kept, value.shape), value, 0.0
                )
            return 0

        lax.fori_loop(0, blocks, smooth, 0)

    source = forces[(PASSES - 1) % 2]

    def finish(i, _):
        at = i * wide
        for c in range(3):
            value = relaxed(source, c, at, TOP, SLAB)
            value = velocity[c, pl.ds(at, wide), TOP:END] - update_rate * value
            for j in range(wide):
                lanes = pl.ds(pl.multiple_of((at + j) * LANES, LANES), LANES)
                out_velocity[0, c, :, lanes] = value[j]
        return 0

    lax.fori_loop(0, blocks, finish, 0)

    for k in range(1, people):
        warp_copy(k).wait_recv()
    for g in range(groups):
        count = jnp.zeros((SLAB, LANES), jnp.float32)
        sums = [jnp.zeros((SLAB, LANES), jnp.float32) for j in range(piece)]
        for t in range(people):
            is_in = jnp.broadcast_to(members[t], (SLAB, LANES)) == g
            count = count + jnp.where(is_in, 1.0, 0.0)
            sums = [sums[j] + jnp.where(is_in, gathered[t, j], 0.0) for j in range(piece)]
        for j in range(piece):
            out_template[g, :, j * LANES : (j + 1) * LANES] = sums[j] / count

    speed_halo[1]()
    warp_halo[1]()
    pick_halo[1]()
    piece_halo[1]()

    @pl.when(is_odd)
    def _():
        for k in order:
            member_copy(k).wait_send()
            mate_copy(k).wait_send()

    for k in order:
        pick_all(k, lambda copy: copy.wait_send())
        warp_copy(k).wait_send()


def place(velocity, template, out_velocity, out_template, sent):
    copies = [
        pltpu.make_async_copy(velocity, out_velocity, sent.at[0]),
        pltpu.make_async_copy(template, out_template, sent.at[1]),
    ]
    for copy in copies:
        copy.start()
    for copy in copies:
        copy.wait()


def local(template, images, speeds, direction, membership):
    groups = template.shape[0]
    people = lax.axis_size("subj")
    slabs = lax.axis_size("space")
    chunks = images.shape[2] // LANES
    piece = chunks // people
    depth = chunks // NH
    vmem = pl.BlockSpec(memory_space=pltpu.VMEM)
    dma = pltpu.SemaphoreType.DMA
    f32 = jnp.float32
    padded = (chunks + 2 * NH, ROWS, LANES)
    results = pl.pallas_call(
        functools.partial(kernel, groups, slabs, people, chunks, piece, depth),
        out_shape=(
            pltpu.VMEM(speeds.shape, f32),
            pltpu.VMEM(template.shape, f32),
        ),
        in_specs=[pl.BlockSpec(memory_space=pl.ANY)] * 5,
        out_specs=(vmem, vmem),
        scratch_shapes=[
            pltpu.VMEM((groups, piece, ROWS, LANES), f32),
            pltpu.VMEM(images.shape, images.dtype),
            pltpu.VMEM(speeds.shape, f32),
            pltpu.VMEM(direction.shape, direction.dtype),
            pltpu.VMEM(membership.shape, membership.dtype),
            dma((4 + piece,)),
            pltpu.VMEM(padded, f32),
            pltpu.VMEM(padded, f32),
            pltpu.VMEM(padded, f32),
            pltpu.VMEM((3, chunks, ROWS, LANES), f32),
            pltpu.VMEM((3,) + padded, f32),
            pltpu.VMEM((3,) + padded, f32),
            pltpu.VMEM((chunks, 2 * PASSES + SLAB, LANES), f32),
            pltpu.VMEM((people, piece, 2 * PASSES + SLAB, LANES), f32),
            pltpu.VMEM((people, piece, SLAB, LANES), f32),
            pltpu.VMEM((people, 1, LANES), jnp.int32),
            dma((10,)), dma((10,)),
            dma((people,)), dma((people,)), dma((people,)),
            dma((people,)), dma((people,)),
            dma((people,)), dma((people,)),
        ],
        compiler_params=pltpu.CompilerParams(collective_id=0, has_side_effects=True),
    )(template, images, speeds, direction, membership)
    return pl.pallas_call(
        place,
        out_shape=(
            jax.ShapeDtypeStruct(speeds.shape, f32),
            jax.ShapeDtypeStruct(template.shape, f32),
        ),
        in_specs=[vmem] * 2,
        out_specs=(pl.BlockSpec(memory_space=pl.ANY),) * 2,
        scratch_shapes=[dma((2,))],
    )(*(pltpu.with_memory_space_constraint(r, pltpu.VMEM) for r in results))


def solution(mesh):
    placed = (
        P(None, "space", "subj"),
        P("subj", "space", None),
        P("subj", None, "space", None),
        P("subj", None, "space", None),
        P("subj", None),
    )
    return jax.shard_map(
        local,
        mesh=mesh,
        in_specs=placed,
        out_specs=(P("subj", None, "space", None), P(None, "space", "subj")),
        check_vma=False,
    )
```

```python
import functools

import jax
import jax.numpy as jnp
from jax import lax
from jax.experimental import pallas as pl
from jax.experimental.pallas import tpu as pltpu
from jax.sharding import PartitionSpec as P

NY = 256
STEPS = 4
PASSES = 4
LANES = 128
SLAB = 8
NH = NY // LANES
ROWS = 3 * SLAB
TOP = SLAB
END = 2 * SLAB
MESH = pl.DeviceIdType.MESH

update_rate = 0.5


def to(axis, index, **other):
    return {"device_id": {axis: index, **other}, "device_id_type": MESH}


def partner(s, k):
    t = s
    bit = 1
    while bit <= k:
        if k & bit:
            t = t + bit - 2 * bit * lax.rem(s // bit, 2)
        bit *= 2
    return t


def beside_in_row(x, depth):
    count, rows, _ = x.shape
    grid = x.reshape(depth, NH, rows, LANES)
    lane = lax.broadcasted_iota(jnp.int32, (depth, rows, LANES), 2)
    up = pltpu.roll(grid, 1, 3)
    down = pltpu.roll(grid, LANES - 1, 3)
    zero = jnp.zeros((depth, rows, LANES), jnp.float32)
    before, after = [], []
    for h in range(NH):
        before.append(jnp.where(lane == 0, up[:, h - 1] if h else zero, up[:, h]))
        after.append(
            jnp.where(lane == LANES - 1, down[:, h + 1] if h + 1 < NH else zero, down[:, h])
        )
    return (
        jnp.stack(before, axis=1).reshape(count, rows, LANES),
        jnp.stack(after, axis=1).reshape(count, rows, LANES),
    )


def kernel(
    groups, slabs, people, chunks, piece, depth,
    template_any, images_any, speeds_any, direction_any, membership_any,
    out_velocity, out_template,
    template, images, speeds, direction, membership, load,
    distant, field_a, field_b, warped, velocity, force_a, force_b, chosen, chosen_out, gathered, members,
    halo_send, halo_recv, member_send, member_recv, mate_send, ready, distant_send, distant_recv, pick_send, pick_recv, warp_send, warp_recv,
):
    p = lax.axis_index("space")
    s = lax.axis_index("subj")
    has_left = p > 0
    has_right = p < slabs - 1
    is_odd = lax.rem(p, 2) == 1
    is_even = jnp.logical_not(is_odd)
    far_left = has_left & is_even
    far_right = has_right & is_odd
    half = people // 2
    barrier = pltpu.get_barrier_semaphore()

    @pl.when(has_left)
    def _():
        pl.semaphore_signal(barrier, 1, **to("space", p - 1))

    @pl.when(has_right)
    def _():
        pl.semaphore_signal(barrier, 1, **to("space", p + 1))

    mirror = partner(s, half)
    pl.semaphore_signal(barrier, 1, **to("subj", mirror))

    @pl.when(is_odd)
    def _():
        for k in range(1, half):
            pl.semaphore_signal(barrier, 1, **to("subj", partner(s, k)))

    @pl.when(far_left)
    def _():
        pl.semaphore_signal(barrier, 1, **to("subj", mirror, space=p - 1))

    @pl.when(far_right)
    def _():
        pl.semaphore_signal(barrier, 1, **to("subj", mirror, space=p + 1))

    loads = [
        pltpu.make_async_copy(source, target, load.at[i])
        for i, (source, target) in enumerate(
            ((membership_any, membership), (images_any, images), (speeds_any, speeds), (direction_any, direction))
        )
    ] + [
        pltpu.make_async_copy(
            template_any.at[:, :, pl.ds(j * LANES, LANES)],
            template.at[:, j, pl.ds(TOP, SLAB)],
            load.at[4 + j],
        )
        for j in range(piece)
    ]
    for copy in loads:
        copy.start()
    inner = slice(NH, NH + chunks)
    wide = depth * NH
    blocks = chunks // wide

    edge = jnp.zeros((NH, ROWS, LANES), jnp.float32)
    for field in (field_a, field_b, warped):
        field[0:NH] = edge
        field[NH + chunks :] = edge
    for field in (force_a, force_b):
        for c in range(3):
            field[c, 0:NH] = edge
            field[c, NH + chunks :] = edge
    outside = jnp.zeros((chunks, SLAB, LANES), jnp.float32)

    def blank(rows):
        field_a[inner, rows] = outside
        warped[inner, rows] = outside
        for held in (template, distant):
            held[:, :, rows] = jnp.zeros((groups, piece, SLAB, LANES), jnp.float32)
        for c in range(3):
            velocity[c, :, rows] = outside

    @pl.when(jnp.logical_not(has_left))
    def _():
        blank(slice(0, TOP))
        chosen[:, 0:PASSES] = outside[:, 0:PASSES]

    @pl.when(jnp.logical_not(has_right))
    def _():
        blank(slice(END, ROWS))
        chosen[:, PASSES + SLAB :] = outside[:, 0:PASSES]

    @pl.when(has_left & is_odd)
    def _():
        for held in (template, distant):
            held[:, :, 0:TOP] = jnp.zeros((groups, piece, SLAB, LANES), jnp.float32)

    @pl.when(has_right & is_even)
    def _():
        for held in (template, distant):
            held[:, :, END:ROWS] = jnp.zeros((groups, piece, SLAB, LANES), jnp.float32)

    for copy in loads:
        copy.wait()
    def unpack(i, _):
        start = pl.multiple_of(i * wide * LANES, LANES)
        block = images[0, :, pl.ds(start, wide * LANES)].astype(jnp.float32)
        for j in range(wide):
            field_a[NH + i * wide + j, TOP:END] = block[:, j * LANES : (j + 1) * LANES]
        for c in range(3):
            sign = (2 * direction[0, c, :, pl.ds(start, wide * LANES)] - 1).astype(jnp.float32)
            signed = sign * speeds[0, c, :, pl.ds(start, wide * LANES)]
            for j in range(wide):
                velocity[c, i * wide + j, TOP:END] = signed[:, j * LANES : (j + 1) * LANES]
        return 0

    lax.fori_loop(0, blocks, unpack, 0)
    members[s] = jnp.broadcast_to(membership[...], (1, LANES))
    near = jnp.where(has_left, 1, 0) + jnp.where(has_right, 1, 0)
    far = jnp.where(far_left | far_right, 1, 0)
    pl.semaphore_wait(barrier, near + far + jnp.where(is_odd, half, 1))

    def halo(number, cut, width, with_left=has_left, with_right=has_right):
        def copy(side, source, target, index):
            return pltpu.make_async_remote_copy(
                src_ref=cut(source), dst_ref=cut(target),
                send_sem=halo_send.at[2 * number + side], recv_sem=halo_recv.at[2 * number + side],
                **to("space", index),
            )

        left = copy(0, TOP, END, p - 1)
        right = copy(1, END - width, TOP - width, p + 1)

        def both(to_left, to_right):
            @pl.when(with_left)
            def _():
                to_left()

            @pl.when(with_right)
            def _():
                to_right()

        start = lambda: both(left.start, right.start)
        sent = lambda: both(left.wait_send, right.wait_send)
        landed = lambda: both(right.wait_recv, left.wait_recv)
        return start, sent, landed

    def member_copy(k):
        return pltpu.make_async_remote_copy(
            src_ref=members.at[s], dst_ref=members.at[s],
            send_sem=member_send.at[k], recv_sem=member_recv.at[k],
            **to("subj", partner(s, k)),
        )

    def mate_copy(k):
        t = partner(s, k)
        return pltpu.make_async_remote_copy(
            src_ref=members.at[t], dst_ref=members.at[t],
            send_sem=mate_send.at[k], recv_sem=member_recv.at[k],
            **to("space", p + 1 - 2 * lax.rem(p, 2)),
        )

    def distant_copy(i, q, source, rows, target):
        return pltpu.make_async_remote_copy(
            src_ref=template.at[:, :, pl.ds(source, rows)],
            dst_ref=distant.at[:, :, pl.ds(target, rows)],
            send_sem=distant_send.at[i], recv_sem=distant_recv.at[i],
            **to("subj", mirror, space=q),
        )

    distant_own = distant_copy(0, p, TOP, SLAB, TOP)
    to_left = distant_copy(1, p - 1, TOP, PASSES, END)
    to_right = distant_copy(1, p + 1, END - PASSES, PASSES, TOP - PASSES)

    def distant_all(act):
        pl.when(far_left)(lambda: act(to_left))
        pl.when(far_right)(lambda: act(to_right))
        act(distant_own)

    def pick_copies(k, which):
        t = partner(s, k)
        owner = mirror if which else s

        def over(first, rows):
            return pltpu.make_async_remote_copy(
                src_ref=chosen_out.at[which, k, :, pl.ds(first, rows)],
                dst_ref=chosen.at[pl.ds(owner * piece, piece), pl.ds(first, rows)],
                send_sem=pick_send.at[which, k], recv_sem=pick_recv.at[which, k],
                **to("subj", t),
            )

        return (
            (far_left, over(0, PASSES + SLAB)),
            (far_right, over(PASSES, PASSES + SLAB)),
            (jnp.logical_not(far_left | far_right), over(PASSES, SLAB)),
        )

    def pick_all(k, which, act):
        for condition, copy in pick_copies(k, which):
            pl.when(condition)(functools.partial(act, copy))

    def pick(k, which):
        held = distant if which else template
        mine = jnp.broadcast_to(members[partner(s, k)], (2 * PASSES + SLAB, LANES))
        for j in range(piece):
            total = jnp.zeros((2 * PASSES + SLAB, LANES), jnp.float32)
            for g in range(groups):
                total = jnp.where(mine == g, held[g, j, TOP - PASSES : END + PASSES], total)
            chosen_out[which, k, j] = total

    def pick_own(which):
        pick(0, which)
        here = pl.ds((mirror if which else s) * piece, piece)
        own = pl.ds(PASSES, SLAB)
        chosen[here, own] = chosen_out[which, 0, :, own]

        @pl.when(far_left)
        def _():
            chosen[here, 0:PASSES] = chosen_out[which, 0, :, 0:PASSES]

        @pl.when(far_right)
        def _():
            chosen[here, PASSES + SLAB :] = chosen_out[which, 0, :, PASSES + SLAB :]

    def warp_copy(k):
        t = partner(s, k)
        return pltpu.make_async_remote_copy(
            src_ref=warped.at[pl.ds(NH + t * piece, piece), pl.ds(TOP, SLAB)],
            dst_ref=gathered.at[s],
            send_sem=warp_send.at[k], recv_sem=warp_recv.at[k],
            **to("subj", t),
        )

    image_halo = halo(0, lambda r: field_a.at[pl.ds(NH, chunks), pl.ds(r, STEPS)], STEPS)
    speed_halo = halo(1, lambda r: velocity.at[:, :, pl.ds(r, STEPS - 1)], STEPS - 1)
    warp_halo = halo(2, lambda r: warped.at[pl.ds(NH, chunks), pl.ds(r, PASSES + 1)], PASSES + 1)
    piece_halo = halo(
        3, lambda r: template.at[:, :, pl.ds(r, PASSES)], PASSES, far_left, far_right
    )
    pick_halo = halo(
        4, lambda r: chosen.at[:, pl.ds(r - PASSES, PASSES)], PASSES,
        has_left & is_odd, has_right & is_even,
    )

    order = range(1, people)
    close = range(1, half)

    @pl.when(is_odd)
    def _():
        for k in close:
            member_copy(k).start()

    distant_all(lambda copy: copy.start())
    piece_halo[0]()
    image_halo[0]()
    speed_halo[0]()
    reach = SLAB // 2

    def advect(source, target, first, rows):
        def block(i, _):
            at = i * wide
            center = source[pl.ds(NH + at, wide), first : first + rows]

            def x(shift):
                return source[pl.ds(NH + at, wide), first + shift : first + shift + rows]

            def z(shift):
                return source[pl.ds(NH + at + shift * NH, wide), first : first + rows]

            def v(c):
                return velocity[c, pl.ds(at, wide), first : first + rows]

            before, after = beside_in_row(center, depth)
            moved = jnp.zeros_like(center)
            for c, (low, high) in enumerate(((x(-1), x(1)), (z(-1), z(1)), (before, after))):
                speed = v(c)
                moved = moved + speed * jnp.where(speed > 0.0, center - low, high - center)
            target[pl.ds(NH + at, wide), first : first + rows] = center - moved
            return 0

        lax.fori_loop(0, blocks, block, 0)

    def pick_each():
        for k in close:
            member_copy(k).wait_recv()

            @pl.when(is_odd)
            def _():
                mate_copy(k).start()

        pl.semaphore_signal(ready, 1, **to("subj", mirror))
        piece_halo[2]()
        for k in close:
            pick(k, 0)
            pick_all(k, 0, lambda copy: copy.start())
        pl.when(far_left)(to_right.wait_recv)
        pl.when(far_right)(to_left.wait_recv)
        distant_own.wait_recv()
        for k in reversed(close):
            pick(k, 1)
            pick_all(k, 1, lambda copy: copy.start())
        pick_own(0)
        pick_own(1)

    def transport():
        image_halo[2]()
        speed_halo[2]()
        fields = (field_a, field_b)
        for step in range(STEPS):
            if step == 1:
                image_halo[1]()
            if step < STEPS - 1:
                advect(fields[step % 2], fields[(step + 1) % 2], TOP - reach, 2 * SLAB)
            else:
                advect(fields[step % 2], warped, TOP, SLAB)
        warp_halo[0]()

    turn = jnp.where(has_left & has_right, 1, 0)

    def phase(i, _):
        pl.when(i == turn)(transport)
        pl.when(i != turn)(pick_each)
        return 0

    lax.fori_loop(0, 2, phase, 0)

    pl.semaphore_wait(ready, 1)
    for k in reversed(order):
        warp_copy(k).start()
        if k not in close:
            member_copy(k).start()
    gathered[s] = warped[pl.ds(NH + s * piece, piece), TOP:END]

    for k in close:
        pick_all(k, 0, lambda copy: copy.wait_recv())
        pick_all(k, 1, lambda copy: copy.wait_recv())
    pick_halo[0]()
    warp_halo[2]()
    pick_halo[2]()

    first, rows = TOP - reach, 2 * SLAB

    def push(i, _):
        at = i * wide
        center = warped[pl.ds(NH + at, wide), first : first + rows]
        before, after = beside_in_row(center, depth)
        half = 0.5 * (center - chosen[pl.ds(at, wide)])
        up = warped[pl.ds(NH + at, wide), first - 1 : first - 1 + rows]
        down = warped[pl.ds(NH + at, wide), first + 1 : first + 1 + rows]
        low = warped[pl.ds(at, wide), first : first + rows]
        high = warped[pl.ds(2 * NH + at, wide), first : first + rows]
        here = pl.ds(NH + at, wide)
        force_a[0, here, first : first + rows] = half * (down - up)
        force_a[1, here, first : first + rows] = half * (high - low)
        force_a[2, here, first : first + rows] = half * (after - before)
        return 0

    lax.fori_loop(0, blocks, push, 0)

    row = lax.broadcasted_iota(jnp.int32, (1, rows, LANES), 1) + first
    lowest = jnp.where(has_left, 0, TOP)
    highest = jnp.where(has_right, ROWS, END)
    kept = (row >= lowest) & (row < highest)

    def relaxed(source, c, at, first, rows):
        center = source[c, pl.ds(NH + at, wide), first : first + rows]
        before, after = beside_in_row(center, depth)
        total = before + after
        total = total + source[c, pl.ds(NH + at, wide), first - 1 : first - 1 + rows]
        total = total + source[c, pl.ds(NH + at, wide), first + 1 : first + 1 + rows]
        total = total + source[c, pl.ds(at, wide), first : first + rows]
        total = total + source[c, pl.ds(2 * NH + at, wide), first : first + rows]
        return 0.25 * center + 0.125 * total

    forces = (force_a, force_b)
    for number in range(PASSES - 1):
        source, target = forces[number % 2], forces[(number + 1) % 2]

        def smooth(i, _, source=source, target=target):
            at = i * wide
            for c in range(3):
                value = relaxed(source, c, at, first, rows)
                target[c, pl.ds(NH + at, wide), first : first + rows] = jnp.where(
                    jnp.broadcast_to(kept, value.shape), value, 0.0
                )
            return 0

        lax.fori_loop(0, blocks, smooth, 0)

    source = forces[(PASSES - 1) % 2]

    def finish(i, _):
        at = i * wide
        for c in range(3):
            value = relaxed(source, c, at, TOP, SLAB)
            value = velocity[c, pl.ds(at, wide), TOP:END] - update_rate * value
            for j in range(wide):
                lanes = pl.ds(pl.multiple_of((at + j) * LANES, LANES), LANES)
                out_velocity[0, c, :, lanes] = value[j]
        return 0

    lax.fori_loop(0, blocks, finish, 0)

    for k in range(1, people):
        warp_copy(k).wait_recv()
        if k not in close:
            member_copy(k).wait_recv()
    for g in range(groups):
        count = jnp.zeros((SLAB, LANES), jnp.float32)
        sums = [jnp.zeros((SLAB, LANES), jnp.float32) for j in range(piece)]
        for t in range(people):
            is_in = jnp.broadcast_to(members[t], (SLAB, LANES)) == g
            count = count + jnp.where(is_in, 1.0, 0.0)
            sums = [sums[j] + jnp.where(is_in, gathered[t, j], 0.0) for j in range(piece)]
        for j in range(piece):
            out_template[g, :, j * LANES : (j + 1) * LANES] = sums[j] / count

    speed_halo[1]()
    warp_halo[1]()
    pick_halo[1]()
    piece_halo[1]()

    distant_all(lambda copy: copy.wait_send())

    @pl.when(is_odd)
    def _():
        for k in close:
            member_copy(k).wait_send()
            mate_copy(k).wait_send()

    for k in order:
        warp_copy(k).wait_send()
        if k not in close:
            member_copy(k).wait_send()
    for k in close:
        pick_all(k, 0, lambda copy: copy.wait_send())
        pick_all(k, 1, lambda copy: copy.wait_send())


def place(velocity, template, out_velocity, out_template, sent):
    copies = [
        pltpu.make_async_copy(velocity, out_velocity, sent.at[0]),
        pltpu.make_async_copy(template, out_template, sent.at[1]),
    ]
    for copy in copies:
        copy.start()
    for copy in copies:
        copy.wait()


def local(template, images, speeds, direction, membership):
    groups = template.shape[0]
    people = lax.axis_size("subj")
    slabs = lax.axis_size("space")
    chunks = images.shape[2] // LANES
    piece = chunks // people
    depth = chunks // NH
    vmem = pl.BlockSpec(memory_space=pltpu.VMEM)
    dma = pltpu.SemaphoreType.DMA
    f32 = jnp.float32
    padded = (chunks + 2 * NH, ROWS, LANES)
    results = pl.pallas_call(
        functools.partial(kernel, groups, slabs, people, chunks, piece, depth),
        out_shape=(
            pltpu.VMEM(speeds.shape, f32),
            pltpu.VMEM(template.shape, f32),
        ),
        in_specs=[pl.BlockSpec(memory_space=pl.ANY)] * 5,
        out_specs=(vmem, vmem),
        scratch_shapes=[
            pltpu.VMEM((groups, piece, ROWS, LANES), f32),
            pltpu.VMEM(images.shape, images.dtype),
            pltpu.VMEM(speeds.shape, f32),
            pltpu.VMEM(direction.shape, direction.dtype),
            pltpu.VMEM(membership.shape, membership.dtype),
            dma((4 + piece,)),
            pltpu.VMEM((groups, piece, ROWS, LANES), f32),
            pltpu.VMEM(padded, f32),
            pltpu.VMEM(padded, f32),
            pltpu.VMEM(padded, f32),
            pltpu.VMEM((3, chunks, ROWS, LANES), f32),
            pltpu.VMEM((3,) + padded, f32),
            pltpu.VMEM((3,) + padded, f32),
            pltpu.VMEM((chunks, 2 * PASSES + SLAB, LANES), f32),
            pltpu.VMEM((2, people // 2, piece, 2 * PASSES + SLAB, LANES), f32),
            pltpu.VMEM((people, piece, SLAB, LANES), f32),
            pltpu.VMEM((people, 1, LANES), jnp.int32),
            dma((10,)), dma((10,)),
            dma((people,)), dma((people,)), dma((people // 2,)), pltpu.SemaphoreType.REGULAR,
            dma((2,)), dma((2,)),
            dma((2, people // 2)), dma((2, people // 2)),
            dma((people,)), dma((people,)),
        ],
        compiler_params=pltpu.CompilerParams(collective_id=0, has_side_effects=True),
    )(template, images, speeds, direction, membership)
    return pl.pallas_call(
        place,
        out_shape=(
            jax.ShapeDtypeStruct(speeds.shape, f32),
            jax.ShapeDtypeStruct(template.shape, f32),
        ),
        in_specs=[vmem] * 2,
        out_specs=(pl.BlockSpec(memory_space=pl.ANY),) * 2,
        scratch_shapes=[dma((2,))],
    )(*(pltpu.with_memory_space_constraint(r, pltpu.VMEM) for r in results))


def solution(mesh):
    placed = (
        P(None, "space", "subj"),
        P("subj", "space", None),
        P("subj", None, "space", None),
        P("subj", None, "space", None),
        P("subj", None),
    )
    return jax.shard_map(
        local,
        mesh=mesh,
        in_specs=placed,
        out_specs=(P("subj", None, "space", None), P(None, "space", "subj")),
        check_vma=False,
    )
```

```python
import functools

import jax
import jax.numpy as jnp
from jax import lax
from jax.experimental import pallas as pl
from jax.experimental.pallas import tpu as pltpu
from jax.sharding import PartitionSpec as P

NY = 256
STEPS = 4
PASSES = 4
LANES = 128
SLAB = 8
NH = NY // LANES
ROWS = 3 * SLAB
TOP = SLAB
END = 2 * SLAB
MESH = pl.DeviceIdType.MESH

update_rate = 0.5


def to(axis, index, **other):
    return {"device_id": {axis: index, **other}, "device_id_type": MESH}


def partner(s, k):
    t = s
    bit = 1
    while bit <= k:
        if k & bit:
            t = t + bit - 2 * bit * lax.rem(s // bit, 2)
        bit *= 2
    return t


def beside_in_row(x, depth):
    count, rows, _ = x.shape
    grid = x.reshape(depth, NH, rows, LANES)
    lane = lax.broadcasted_iota(jnp.int32, (depth, rows, LANES), 2)
    up = pltpu.roll(grid, 1, 3)
    down = pltpu.roll(grid, LANES - 1, 3)
    zero = jnp.zeros((depth, rows, LANES), jnp.float32)
    before, after = [], []
    for h in range(NH):
        before.append(jnp.where(lane == 0, up[:, h - 1] if h else zero, up[:, h]))
        after.append(
            jnp.where(lane == LANES - 1, down[:, h + 1] if h + 1 < NH else zero, down[:, h])
        )
    return (
        jnp.stack(before, axis=1).reshape(count, rows, LANES),
        jnp.stack(after, axis=1).reshape(count, rows, LANES),
    )


def kernel(
    groups, slabs, people, chunks, piece, depth,
    template_any, images_any, speeds_any, direction_any, membership_any,
    out_velocity, out_template,
    template, images, speeds, direction, membership, load,
    distant, field_a, field_b, warped, velocity, force_a, force_b, chosen, chosen_out, gathered, members,
    halo_send, halo_recv, member_send, member_recv, mate_send, ready, distant_send, distant_recv, pick_send, pick_recv, warp_send, warp_recv,
):
    p = lax.axis_index("space")
    s = lax.axis_index("subj")
    has_left = p > 0
    has_right = p < slabs - 1
    is_odd = lax.rem(p, 2) == 1
    is_even = jnp.logical_not(is_odd)
    far_left = has_left & is_even
    far_right = has_right & is_odd
    half = people // 2
    barrier = pltpu.get_barrier_semaphore()

    @pl.when(has_left)
    def _():
        pl.semaphore_signal(barrier, 1, **to("space", p - 1))

    @pl.when(has_right)
    def _():
        pl.semaphore_signal(barrier, 1, **to("space", p + 1))

    mirror = partner(s, half)
    is_lower = s < half
    is_upper = jnp.logical_not(is_lower)
    pl.semaphore_signal(barrier, 1, **to("subj", mirror))

    @pl.when(is_odd)
    def _():
        for k in range(1, half):
            pl.semaphore_signal(barrier, 1, **to("subj", partner(s, k)))

    @pl.when(is_lower & far_left)
    def _():
        pl.semaphore_signal(barrier, 1, **to("subj", mirror, space=p - 1))

    @pl.when(is_lower & far_right)
    def _():
        pl.semaphore_signal(barrier, 1, **to("subj", mirror, space=p + 1))

    loads = [
        pltpu.make_async_copy(source, target, load.at[i])
        for i, (source, target) in enumerate(
            ((membership_any, membership), (images_any, images), (speeds_any, speeds), (direction_any, direction))
        )
    ] + [
        pltpu.make_async_copy(
            template_any.at[:, :, pl.ds(j * LANES, LANES)],
            template.at[:, j, pl.ds(TOP, SLAB)],
            load.at[4 + j],
        )
        for j in range(piece)
    ]
    for copy in loads:
        copy.start()
    inner = slice(NH, NH + chunks)
    wide = depth * NH
    blocks = chunks // wide

    edge = jnp.zeros((NH, ROWS, LANES), jnp.float32)
    for field in (field_a, field_b, warped):
        field[0:NH] = edge
        field[NH + chunks :] = edge
    for field in (force_a, force_b):
        for c in range(3):
            field[c, 0:NH] = edge
            field[c, NH + chunks :] = edge
    outside = jnp.zeros((chunks, SLAB, LANES), jnp.float32)

    def blank(rows):
        field_a[inner, rows] = outside
        warped[inner, rows] = outside
        for held in (template, distant):
            held[:, :, rows] = jnp.zeros((groups, piece, SLAB, LANES), jnp.float32)
        for c in range(3):
            velocity[c, :, rows] = outside

    @pl.when(jnp.logical_not(has_left))
    def _():
        blank(slice(0, TOP))
        chosen[:, 0:PASSES] = outside[:, 0:PASSES]

    @pl.when(jnp.logical_not(has_right))
    def _():
        blank(slice(END, ROWS))
        chosen[:, PASSES + SLAB :] = outside[:, 0:PASSES]

    @pl.when(has_left & is_odd)
    def _():
        for held in (template, distant):
            held[:, :, 0:TOP] = jnp.zeros((groups, piece, SLAB, LANES), jnp.float32)

    @pl.when(has_right & is_even)
    def _():
        for held in (template, distant):
            held[:, :, END:ROWS] = jnp.zeros((groups, piece, SLAB, LANES), jnp.float32)

    for copy in loads:
        copy.wait()
    def unpack(i, _):
        start = pl.multiple_of(i * wide * LANES, LANES)
        block = images[0, :, pl.ds(start, wide * LANES)].astype(jnp.float32)
        for j in range(wide):
            field_a[NH + i * wide + j, TOP:END] = block[:, j * LANES : (j + 1) * LANES]
        for c in range(3):
            sign = (2 * direction[0, c, :, pl.ds(start, wide * LANES)] - 1).astype(jnp.float32)
            signed = sign * speeds[0, c, :, pl.ds(start, wide * LANES)]
            for j in range(wide):
                velocity[c, i * wide + j, TOP:END] = signed[:, j * LANES : (j + 1) * LANES]
        return 0

    lax.fori_loop(0, blocks, unpack, 0)
    members[s] = jnp.broadcast_to(membership[...], (1, LANES))
    near = jnp.where(has_left, 1, 0) + jnp.where(has_right, 1, 0)
    far = jnp.where(is_upper & (far_left | far_right), 1, 0)
    pl.semaphore_wait(barrier, near + far + jnp.where(is_odd, half, 1))

    def halo(number, cut, width, with_left=has_left, with_right=has_right):
        def copy(side, source, target, index):
            return pltpu.make_async_remote_copy(
                src_ref=cut(source), dst_ref=cut(target),
                send_sem=halo_send.at[2 * number + side], recv_sem=halo_recv.at[2 * number + side],
                **to("space", index),
            )

        left = copy(0, TOP, END, p - 1)
        right = copy(1, END - width, TOP - width, p + 1)

        def both(to_left, to_right):
            @pl.when(with_left)
            def _():
                to_left()

            @pl.when(with_right)
            def _():
                to_right()

        start = lambda: both(left.start, right.start)
        sent = lambda: both(left.wait_send, right.wait_send)
        landed = lambda: both(right.wait_recv, left.wait_recv)
        return start, sent, landed

    def member_copy(k):
        return pltpu.make_async_remote_copy(
            src_ref=members.at[s], dst_ref=members.at[s],
            send_sem=member_send.at[k], recv_sem=member_recv.at[k],
            **to("subj", partner(s, k)),
        )

    def mate_copy(k):
        t = partner(s, k)
        return pltpu.make_async_remote_copy(
            src_ref=members.at[t], dst_ref=members.at[t],
            send_sem=mate_send.at[k], recv_sem=member_recv.at[k],
            **to("space", p + 1 - 2 * lax.rem(p, 2)),
        )

    def distant_copy(i, q, source, rows, target):
        return pltpu.make_async_remote_copy(
            src_ref=template.at[:, :, pl.ds(source, rows)],
            dst_ref=distant.at[:, :, pl.ds(target, rows)],
            send_sem=distant_send.at[i], recv_sem=distant_recv.at[i],
            **to("subj", mirror, space=q),
        )

    distant_own = distant_copy(0, p, TOP, SLAB, TOP)
    to_left = distant_copy(1, p - 1, TOP, PASSES, END)
    to_right = distant_copy(1, p + 1, END - PASSES, PASSES, TOP - PASSES)

    wide_left = distant_copy(0, p, TOP - PASSES, PASSES + SLAB, TOP - PASSES)
    wide_right = distant_copy(0, p, TOP, PASSES + SLAB, TOP)
    alone = jnp.logical_not(far_left | far_right)

    def distant_narrow(with_own, with_far, left, right, act):
        pl.when(with_far & far_left)(lambda: act(left))
        pl.when(with_far & far_right)(lambda: act(right))
        pl.when(with_own | alone)(lambda: act(distant_own))

    def distant_wide(side, act):
        pl.when(side & far_left)(lambda: act(wide_left))
        pl.when(side & far_right)(lambda: act(wide_right))

    def pick_copies(k, which):
        t = partner(s, k)
        owner = mirror if which else s

        def over(first, rows):
            return pltpu.make_async_remote_copy(
                src_ref=chosen_out.at[which, k, :, pl.ds(first, rows)],
                dst_ref=chosen.at[pl.ds(owner * piece, piece), pl.ds(first, rows)],
                send_sem=pick_send.at[which, k], recv_sem=pick_recv.at[which, k],
                **to("subj", t),
            )

        return (
            (far_left, over(0, PASSES + SLAB)),
            (far_right, over(PASSES, PASSES + SLAB)),
            (jnp.logical_not(far_left | far_right), over(PASSES, SLAB)),
        )

    def pick_all(k, which, act):
        for condition, copy in pick_copies(k, which):
            pl.when(condition)(functools.partial(act, copy))

    def pick(k, which):
        held = distant if which else template
        mine = jnp.broadcast_to(members[partner(s, k)], (2 * PASSES + SLAB, LANES))
        for j in range(piece):
            total = jnp.zeros((2 * PASSES + SLAB, LANES), jnp.float32)
            for g in range(groups):
                total = jnp.where(mine == g, held[g, j, TOP - PASSES : END + PASSES], total)
            chosen_out[which, k, j] = total

    def pick_own(which):
        pick(0, which)
        here = pl.ds((mirror if which else s) * piece, piece)
        own = pl.ds(PASSES, SLAB)
        chosen[here, own] = chosen_out[which, 0, :, own]

        @pl.when(far_left)
        def _():
            chosen[here, 0:PASSES] = chosen_out[which, 0, :, 0:PASSES]

        @pl.when(far_right)
        def _():
            chosen[here, PASSES + SLAB :] = chosen_out[which, 0, :, PASSES + SLAB :]

    def warp_copy(k):
        t = partner(s, k)
        return pltpu.make_async_remote_copy(
            src_ref=warped.at[pl.ds(NH + t * piece, piece), pl.ds(TOP, SLAB)],
            dst_ref=gathered.at[s],
            send_sem=warp_send.at[k], recv_sem=warp_recv.at[k],
            **to("subj", t),
        )

    image_halo = halo(0, lambda r: field_a.at[pl.ds(NH, chunks), pl.ds(r, STEPS)], STEPS)
    speed_halo = halo(1, lambda r: velocity.at[:, :, pl.ds(r, STEPS - 1)], STEPS - 1)
    warp_halo = halo(2, lambda r: warped.at[pl.ds(NH, chunks), pl.ds(r, PASSES + 1)], PASSES + 1)
    piece_halo = halo(
        3, lambda r: template.at[:, :, pl.ds(r, PASSES)], PASSES, far_left, far_right
    )
    pick_halo = halo(
        4, lambda r: chosen.at[:, pl.ds(r - PASSES, PASSES)], PASSES,
        has_left & is_odd, has_right & is_even,
    )

    order = range(1, people)
    close = range(1, half)

    @pl.when(is_odd)
    def _():
        for k in close:
            member_copy(k).start()

    distant_narrow(is_upper, is_upper, to_left, to_right, lambda copy: copy.start())
    piece_halo[0]()
    image_halo[0]()
    speed_halo[0]()
    reach = SLAB // 2

    def advect(source, target, first, rows):
        def block(i, _):
            at = i * wide
            center = source[pl.ds(NH + at, wide), first : first + rows]

            def x(shift):
                return source[pl.ds(NH + at, wide), first + shift : first + shift + rows]

            def z(shift):
                return source[pl.ds(NH + at + shift * NH, wide), first : first + rows]

            def v(c):
                return velocity[c, pl.ds(at, wide), first : first + rows]

            before, after = beside_in_row(center, depth)
            moved = jnp.zeros_like(center)
            for c, (low, high) in enumerate(((x(-1), x(1)), (z(-1), z(1)), (before, after))):
                speed = v(c)
                moved = moved + speed * jnp.where(speed > 0.0, center - low, high - center)
            target[pl.ds(NH + at, wide), first : first + rows] = center - moved
            return 0

        lax.fori_loop(0, blocks, block, 0)

    def pick_each():
        piece_halo[2]()
        distant_wide(is_lower, lambda copy: copy.start())
        for k in close:
            member_copy(k).wait_recv()

            @pl.when(is_odd)
            def _():
                mate_copy(k).start()

        pl.semaphore_signal(ready, 1, **to("subj", mirror))
        for k in close:
            pick(k, 0)
            pick_all(k, 0, lambda copy: copy.start())
        distant_narrow(is_lower, is_lower, to_right, to_left, lambda copy: copy.wait_recv())
        distant_wide(is_upper, lambda copy: copy.wait_recv())
        for k in reversed(close):
            pick(k, 1)
            pick_all(k, 1, lambda copy: copy.start())
        pick_own(0)
        pick_own(1)

    def transport():
        image_halo[2]()
        speed_halo[2]()
        fields = (field_a, field_b)
        for step in range(STEPS):
            if step == 1:
                image_halo[1]()
            if step < STEPS - 1:
                advect(fields[step % 2], fields[(step + 1) % 2], TOP - reach, 2 * SLAB)
            else:
                advect(fields[step % 2], warped, TOP, SLAB)
        warp_halo[0]()

    turn = jnp.where(has_left & has_right, 1, 0)

    def phase(i, _):
        pl.when(i == turn)(transport)
        pl.when(i != turn)(pick_each)
        return 0

    lax.fori_loop(0, 2, phase, 0)

    pl.semaphore_wait(ready, 1)
    for k in reversed(order):
        warp_copy(k).start()
        if k not in close:
            member_copy(k).start()
    gathered[s] = warped[pl.ds(NH + s * piece, piece), TOP:END]

    for k in close:
        pick_all(k, 0, lambda copy: copy.wait_recv())
        pick_all(k, 1, lambda copy: copy.wait_recv())
    pick_halo[0]()
    warp_halo[2]()
    pick_halo[2]()

    first, rows = TOP - reach, 2 * SLAB

    def push(i, _):
        at = i * wide
        center = warped[pl.ds(NH + at, wide), first : first + rows]
        before, after = beside_in_row(center, depth)
        half = 0.5 * (center - chosen[pl.ds(at, wide)])
        up = warped[pl.ds(NH + at, wide), first - 1 : first - 1 + rows]
        down = warped[pl.ds(NH + at, wide), first + 1 : first + 1 + rows]
        low = warped[pl.ds(at, wide), first : first + rows]
        high = warped[pl.ds(2 * NH + at, wide), first : first + rows]
        here = pl.ds(NH + at, wide)
        force_a[0, here, first : first + rows] = half * (down - up)
        force_a[1, here, first : first + rows] = half * (high - low)
        force_a[2, here, first : first + rows] = half * (after - before)
        return 0

    lax.fori_loop(0, blocks, push, 0)

    row = lax.broadcasted_iota(jnp.int32, (1, rows, LANES), 1) + first
    lowest = jnp.where(has_left, 0, TOP)
    highest = jnp.where(has_right, ROWS, END)
    kept = (row >= lowest) & (row < highest)

    def relaxed(source, c, at, first, rows):
        center = source[c, pl.ds(NH + at, wide), first : first + rows]
        before, after = beside_in_row(center, depth)
        total = before + after
        total = total + source[c, pl.ds(NH + at, wide), first - 1 : first - 1 + rows]
        total = total + source[c, pl.ds(NH + at, wide), first + 1 : first + 1 + rows]
        total = total + source[c, pl.ds(at, wide), first : first + rows]
        total = total + source[c, pl.ds(2 * NH + at, wide), first : first + rows]
        return 0.25 * center + 0.125 * total

    forces = (force_a, force_b)
    for number in range(PASSES - 1):
        source, target = forces[number % 2], forces[(number + 1) % 2]

        def smooth(i, _, source=source, target=target):
            at = i * wide
            for c in range(3):
                value = relaxed(source, c, at, first, rows)
                target[c, pl.ds(NH + at, wide), first : first + rows] = jnp.where(
                    jnp.broadcast_to(kept, value.shape), value, 0.0
                )
            return 0

        lax.fori_loop(0, blocks, smooth, 0)

    source = forces[(PASSES - 1) % 2]

    def finish(i, _):
        at = i * wide
        for c in range(3):
            value = relaxed(source, c, at, TOP, SLAB)
            value = velocity[c, pl.ds(at, wide), TOP:END] - update_rate * value
            for j in range(wide):
                lanes = pl.ds(pl.multiple_of((at + j) * LANES, LANES), LANES)
                out_velocity[0, c, :, lanes] = value[j]
        return 0

    lax.fori_loop(0, blocks, finish, 0)

    for k in range(1, people):
        warp_copy(k).wait_recv()
        if k not in close:
            member_copy(k).wait_recv()
    for g in range(groups):
        count = jnp.zeros((SLAB, LANES), jnp.float32)
        sums = [jnp.zeros((SLAB, LANES), jnp.float32) for j in range(piece)]
        for t in range(people):
            is_in = jnp.broadcast_to(members[t], (SLAB, LANES)) == g
            count = count + jnp.where(is_in, 1.0, 0.0)
            sums = [sums[j] + jnp.where(is_in, gathered[t, j], 0.0) for j in range(piece)]
        for j in range(piece):
            out_template[g, :, j * LANES : (j + 1) * LANES] = sums[j] / count

    speed_halo[1]()
    warp_halo[1]()
    pick_halo[1]()
    piece_halo[1]()

    distant_narrow(is_upper, is_upper, to_left, to_right, lambda copy: copy.wait_send())
    distant_wide(is_lower, lambda copy: copy.wait_send())

    @pl.when(is_odd)
    def _():
        for k in close:
            member_copy(k).wait_send()
            mate_copy(k).wait_send()

    for k in order:
        warp_copy(k).wait_send()
        if k not in close:
            member_copy(k).wait_send()
    for k in close:
        pick_all(k, 0, lambda copy: copy.wait_send())
        pick_all(k, 1, lambda copy: copy.wait_send())


def place(velocity, template, out_velocity, out_template, sent):
    copies = [
        pltpu.make_async_copy(velocity, out_velocity, sent.at[0]),
        pltpu.make_async_copy(template, out_template, sent.at[1]),
    ]
    for copy in copies:
        copy.start()
    for copy in copies:
        copy.wait()


def local(template, images, speeds, direction, membership):
    groups = template.shape[0]
    people = lax.axis_size("subj")
    slabs = lax.axis_size("space")
    chunks = images.shape[2] // LANES
    piece = chunks // people
    depth = chunks // NH
    vmem = pl.BlockSpec(memory_space=pltpu.VMEM)
    dma = pltpu.SemaphoreType.DMA
    f32 = jnp.float32
    padded = (chunks + 2 * NH, ROWS, LANES)
    results = pl.pallas_call(
        functools.partial(kernel, groups, slabs, people, chunks, piece, depth),
        out_shape=(
            pltpu.VMEM(speeds.shape, f32),
            pltpu.VMEM(template.shape, f32),
        ),
        in_specs=[pl.BlockSpec(memory_space=pl.ANY)] * 5,
        out_specs=(vmem, vmem),
        scratch_shapes=[
            pltpu.VMEM((groups, piece, ROWS, LANES), f32),
            pltpu.VMEM(images.shape, images.dtype),
            pltpu.VMEM(speeds.shape, f32),
            pltpu.VMEM(direction.shape, direction.dtype),
            pltpu.VMEM(membership.shape, membership.dtype),
            dma((4 + piece,)),
            pltpu.VMEM((groups, piece, ROWS, LANES), f32),
            pltpu.VMEM(padded, f32),
            pltpu.VMEM(padded, f32),
            pltpu.VMEM(padded, f32),
            pltpu.VMEM((3, chunks, ROWS, LANES), f32),
            pltpu.VMEM((3,) + padded, f32),
            pltpu.VMEM((3,) + padded, f32),
            pltpu.VMEM((chunks, 2 * PASSES + SLAB, LANES), f32),
            pltpu.VMEM((2, people // 2, piece, 2 * PASSES + SLAB, LANES), f32),
            pltpu.VMEM((people, piece, SLAB, LANES), f32),
            pltpu.VMEM((people, 1, LANES), jnp.int32),
            dma((10,)), dma((10,)),
            dma((people,)), dma((people,)), dma((people // 2,)), pltpu.SemaphoreType.REGULAR,
            dma((2,)), dma((2,)),
            dma((2, people // 2)), dma((2, people // 2)),
            dma((people,)), dma((people,)),
        ],
        compiler_params=pltpu.CompilerParams(collective_id=0, has_side_effects=True),
    )(template, images, speeds, direction, membership)
    return pl.pallas_call(
        place,
        out_shape=(
            jax.ShapeDtypeStruct(speeds.shape, f32),
            jax.ShapeDtypeStruct(template.shape, f32),
        ),
        in_specs=[vmem] * 2,
        out_specs=(pl.BlockSpec(memory_space=pl.ANY),) * 2,
        scratch_shapes=[dma((2,))],
    )(*(pltpu.with_memory_space_constraint(r, pltpu.VMEM) for r in results))


def solution(mesh):
    placed = (
        P(None, "space", "subj"),
        P("subj", "space", None),
        P("subj", None, "space", None),
        P("subj", None, "space", None),
        P("subj", None),
    )
    return jax.shard_map(
        local,
        mesh=mesh,
        in_specs=placed,
        out_specs=(P("subj", None, "space", None), P(None, "space", "subj")),
        check_vma=False,
    )
```
